1024 devices in a mesh: outer: 64 (over y_hi, z, core), inner: 16 (over y_lo, x).
Axes of the slice: x: 4, y: 8 (y_hi: 2, y_lo: 4; y = y_hi * 4 + y_lo), z: 16, core: 2. Of those that a mesh axis runs over, the one named last changes fastest.
Arguments:
- queries: bfloat16 [131072, 4096], P(('outer', 'inner')), may hold values from -8 to 8
- keys: bfloat16 [131072, 512], P(('outer', 'inner')), may hold values from -8 to 8
- values: bfloat16 [131072, 512], P(('outer', 'inner')), may hold values from -6 to 6
- acc_out: bfloat16 [131072, 4096], P(('outer', 'inner')), may hold values from -6 to 6
- acc_max: float32 [131072, 32], P(('outer', 'inner')), may hold values from 2 to 4
- acc_sum: float32 [131072, 32], P(('outer', 'inner')), may hold values from 16 to 256
- doc_lengths: int32 [128], replicated, may hold values from 1 to 8192, as said below
Outputs:
- new_out: bfloat16 [131072, 4096], P(('outer', 'inner'))
- new_max: float32 [131072, 32], P(('outer', 'inner'))
- new_sum: float32 [131072, 32], P(('outer', 'inner'))
The draws below stay inside these ranges and needn't reach their ends.
Inputs may be any that keep to these rules, and one draw needn't show every extreme that they name: `doc_lengths`: the lengths add up to 131072; one document is exactly 8192 long and none is longer.
All inputs are finite; a program needn't handle non-finite values.
Results may differ from the reference program's by a relative error of at most 0.0014.
Values may be sent and summed in bfloat16 or wider, within the bound.
A program may use at most 32 MiB of HBM per device.

```python
import math
import jax
import jax.numpy as jnp
from jax import lax

TOK_DEV = 128
HQ = 32
KVH = 4
HD = 128
TOKENS = 131072
BLOCK = 2048
DOCS = 128
DOC_MOST = 8192
N_OUTER = 64
N_INNER = 16


def draw_queries(key, part):
    group = HQ // KVH
    shape = (TOKENS, KVH, group, HD)
    result = jnp.clip(jax.random.normal(jax.random.fold_in(key, 1), shape, jnp.float32), -6.0, 6.0)
    return jnp.clip(result, -8.0, 8.0).reshape(TOKENS, HQ * HD).astype(jnp.bfloat16)


def draw_keys(key, part):
    shape = (TOKENS, KVH, HD)
    result = jnp.clip(jax.random.normal(jax.random.fold_in(key, 21), shape, jnp.float32), -6.0, 6.0)
    return jnp.clip(result, -8.0, 8.0).reshape(TOKENS, KVH * HD).astype(jnp.bfloat16)


def draw_doc_lengths(key, part):
    long_count = max(2, DOCS // 16)
    others = DOCS - long_count
    long_sizes = jax.random.randint(jax.random.fold_in(key, 32), (long_count - 1,), BLOCK // 2, 2 * BLOCK + 1).astype(jnp.int32)
    long_part = jnp.concatenate([jnp.full((1,), DOC_MOST, jnp.int32), long_sizes]).astype(jnp.int32)
    remain = (TOKENS - jnp.sum(long_part)).astype(jnp.int32)
    base_len = (remain // others).astype(jnp.int32)
    leftover = (remain - base_len * others).astype(jnp.int32)
    index_row = jnp.arange(others, dtype=jnp.int32)
    even_share = (base_len + (index_row < leftover).astype(jnp.int32)).astype(jnp.int32)
    pair_count = others // 2
    moving_amount = jax.random.randint(jax.random.fold_in(key, 31), (pair_count,), 0, base_len).astype(jnp.int32)
    changes = jnp.stack([moving_amount, -moving_amount], axis=1).reshape(2 * pair_count)
    changes = jnp.concatenate([changes, jnp.zeros((others - 2 * pair_count,), jnp.int32)]).astype(jnp.int32)
    short_part = (even_share + changes).astype(jnp.int32)
    combined = jnp.concatenate([long_part, short_part]).astype(jnp.int32)
    placing = jax.random.permutation(jax.random.fold_in(key, 33), DOCS)
    return jnp.zeros((DOCS,), jnp.int32).at[placing].set(combined).astype(jnp.int32)


def block_levels(key, shape, cuts, least, largest):
    factor_of, own = 1.0, jax.random.fold_in(key, 6)
    for position, blocks in cuts:
        heights = jnp.exp(jax.random.uniform(jax.random.fold_in(own, position), (blocks,), jnp.float32, least / len(cuts), largest / len(cuts)))
        factor_of = factor_of * jnp.repeat(heights, shape[position] // blocks).reshape([-1 if axis == position else 1 for axis in range(len(shape))])
    return factor_of


def scatter_about(stream_key, shape, scale, reach, pieces=(), kind=jnp.bfloat16):
    level = block_levels(stream_key, shape, pieces, -0.22, 0.18) if pieces else 1.0
    array = jax.random.normal(stream_key, shape, jnp.float32) * scale * level
    return jnp.minimum(jnp.maximum(array, -reach), reach).astype(kind)


def setup_inputs(seed: int = 0) -> dict:
    key_list = jax.random.split(jax.random.key(seed), 8)
    queries = draw_queries(jax.random.fold_in(key_list[7], 71), 0)
    keys = draw_keys(jax.random.fold_in(key_list[7], 71), 0)
    values = scatter_about(key_list[2], (TOKENS, KVH * HD), 1.0, 6.0, ((0, 1024),))
    acc_out = scatter_about(key_list[3], (TOKENS, HQ * HD), 1.0, 6.0, ((0, 1024),))
    acc_max = jnp.clip(2.0 + 2.0 * jax.random.uniform(key_list[4], (TOKENS, HQ), jnp.float32) ** block_levels(key_list[4], (TOKENS, HQ), ((0, 1024),), -0.2, 0.2), 2.0, 4.0)
    acc_sum = jnp.clip(jnp.exp(math.log(256.0) - 2.7725887 * jax.random.uniform(key_list[5], (TOKENS, HQ), jnp.float32) ** block_levels(key_list[5], (TOKENS, HQ), ((0, 1024),), -0.2, 0.2)), 16.0, 256.0)
    doc_lengths = draw_doc_lengths(jax.random.fold_in(key_list[7], 71), 0)
    return dict(queries=queries, keys=keys, values=values, acc_out=acc_out, acc_max=acc_max, acc_sum=acc_sum, doc_lengths=doc_lengths)


NEG = -1e+30

def reference(queries, keys, values, acc_out, acc_max, acc_sum, doc_lengths):
    group = HQ // KVH
    scale = 1.0 / math.sqrt(HD)
    ends = jnp.cumsum(doc_lengths).astype(jnp.int32)
    starts = (ends - doc_lengths).astype(jnp.int32)

    def tile(index):
        first = (index * TOK_DEV).astype(jnp.int32)
        k_block = ((index // N_INNER + N_OUTER - 1) % N_OUTER).astype(jnp.int32)
        k_first = (k_block * BLOCK).astype(jnp.int32)
        q_rows = lax.dynamic_slice_in_dim(queries, first, TOK_DEV, 0).astype(jnp.float32).reshape(TOK_DEV, KVH, group, HD)
        k_rows = lax.dynamic_slice_in_dim(keys, k_first, BLOCK, 0).astype(jnp.float32).reshape(BLOCK, KVH, HD)
        v_rows = lax.dynamic_slice_in_dim(values, k_first, BLOCK, 0).astype(jnp.float32).reshape(BLOCK, KVH, HD)
        qpos = first + jnp.arange(TOK_DEV, dtype=jnp.int32)
        kpos = k_first + jnp.arange(BLOCK, dtype=jnp.int32)
        qstart = lax.optimization_barrier(jnp.max(jnp.where(starts[None, :] <= qpos[:, None], starts[None, :], 0), axis=1))
        visible = (kpos[None, :] <= qpos[:, None]) & (kpos[None, :] >= qstart[:, None])
        keep = visible[:, None, None, :]
        scores = jnp.einsum('rhgd,nhd->rhgn', q_rows, k_rows) * scale
        scores = jnp.where(keep, scores, NEG)
        old_max = lax.dynamic_slice_in_dim(acc_max, first, TOK_DEV, 0).reshape(TOK_DEV, KVH, group)
        old_sum = lax.dynamic_slice_in_dim(acc_sum, first, TOK_DEV, 0).reshape(TOK_DEV, KVH, group)
        top = jnp.maximum(old_max, lax.optimization_barrier(jnp.max(scores, axis=-1)))
        weights = jnp.where(keep, jnp.exp(scores - top[..., None]), 0.0)
        kept = old_sum * jnp.exp(old_max - top)
        total = kept + lax.optimization_barrier(jnp.sum(weights, axis=-1))
        low = lax.optimization_barrier(weights.astype(jnp.bfloat16))
        mixed = jnp.einsum('rhgn,nhd->rhgd', low.astype(jnp.float32), v_rows)
        old_out = lax.dynamic_slice_in_dim(acc_out, first, TOK_DEV, 0).astype(jnp.float32).reshape(TOK_DEV, KVH, group, HD)
        result = (old_out * kept[..., None] + mixed) / total[..., None]
        return (result.reshape(TOK_DEV, HQ * HD).astype(jnp.bfloat16), top.reshape(TOK_DEV, HQ), total.reshape(TOK_DEV, HQ))
    outs = lax.map(tile, jnp.arange(TOKENS // TOK_DEV, dtype=jnp.int32))
    return (outs[0].reshape(TOKENS, HQ * HD), outs[1].reshape(TOKENS, HQ), outs[2].reshape(TOKENS, HQ))
```

```python
import functools
import math

import jax
import jax.numpy as jnp
from jax import lax
from jax.experimental import pallas as pl
from jax.experimental.pallas import tpu as pltpu
from jax.sharding import PartitionSpec as P

HD = 128
NEG = -1e30
LOG2E = math.log2(math.e)
MESH = pl.DeviceIdType.MESH
NX = 4
NY = 4


def kernel(
    q_hbm, k_hbm, v_hbm, ao_hbm, am_hbm, as_hbm, dl_hbm,
    o_hbm, nm_hbm, ns_hbm,
    qs, aos, ams, ass, dls, kbuf, vbuf, acc, m_ref, l_ref, bias, thr,
    in_sem, q_sem, recv_sem, z_sem, y_sem, x_sem, f_sem, out_sem,
):
    rows = k_hbm.shape[0]
    kv_heads = k_hbm.shape[1] // HD
    heads = q_hbm.shape[1] // HD
    group = heads // kv_heads
    wide = group * rows
    n_outer = lax.axis_size("outer")
    half_outer = n_outer // 2
    b = lax.axis_index("outer")
    inner = lax.axis_index("inner")
    y = inner // NX
    x = inner % NX
    xr = (x + 1) % NX
    xl = (x + NX - 1) % NX
    xo = (x + 2) % NX
    nxt = (b + 1) % n_outer
    prv = (b + n_outer - 1) % n_outer
    turn_out = nxt % half_outer == 0
    turn_in = b % half_outer == 0
    y_out = jnp.where(turn_out, NY - 1 - y, y)
    y_in = jnp.where(turn_in, NY - 1 - y, y)
    has_up = y < NY - 1
    has_down = y > 0

    loads = [
        pltpu.make_async_copy(dl_hbm, dls, in_sem.at[0]),
        pltpu.make_async_copy(am_hbm, ams, in_sem.at[1]),
        pltpu.make_async_copy(as_hbm, ass, in_sem.at[2]),
        pltpu.make_async_copy(ao_hbm, aos, in_sem.at[3]),
    ]
    for copy in loads:
        copy.start()
    q_loads = []
    for h in range(heads):
        q_loads.append(
            pltpu.make_async_copy(
                q_hbm.at[:, pl.ds(h * HD, HD)],
                qs.at[h // group, pl.ds((h % group) * rows, rows), :],
                q_sem.at[h],
            )
        )
        q_loads[-1].start()

    barrier = pltpu.get_barrier_semaphore()

    def greet(device):
        pl.semaphore_signal(barrier, inc=1, device_id=device, device_id_type=MESH)

    greet((prv, y_in * NX + x))
    greet((b, y * NX + xr))
    greet((b, y * NX + xl))

    @pl.when(has_up)
    def _():
        greet((b, (y + 1) * NX + x))

    @pl.when(has_down)
    def _():
        greet((b, (y - 1) * NX + x))

    pl.semaphore_wait(barrier, 3 + has_up.astype(jnp.int32) + has_down.astype(jnp.int32))

    bufs = (kbuf, vbuf)
    sources = (k_hbm, v_hbm)

    z_copies = [
        pltpu.make_async_remote_copy(
            src_ref=sources[kv],
            dst_ref=bufs[kv].at[x, y_out],
            send_sem=z_sem.at[kv],
            recv_sem=recv_sem.at[kv, x, y_out],
            device_id=(nxt, y_out * NX + x),
            device_id_type=MESH,
        )
        for kv in range(2)
    ]
    for copy in z_copies:
        copy.start()

    def forward(kv, cx, cy, sem, device):
        return pltpu.make_async_remote_copy(
            src_ref=bufs[kv].at[cx, cy],
            dst_ref=bufs[kv].at[cx, cy],
            send_sem=sem,
            recv_sem=recv_sem.at[kv, cx, cy],
            device_id=device,
            device_id_type=MESH,
        )

    def arrived(kv, cx, cy):
        pltpu.make_async_copy(
            bufs[kv].at[cx, cy], bufs[kv].at[cx, cy], recv_sem.at[kv, cx, cy]
        ).wait()

    def pick(values):
        return jnp.where(
            y == 0, values[0], jnp.where(y == 1, values[1], jnp.where(y == 2, values[2], values[3]))
        )

    order = (y, pick((1, 0, 3, 2)), pick((2, 2, 1, 1)), pick((3, 3, 0, 0)))
    pending = []

    def send(copy, when=None):
        if when is None:
            copy.start()
        else:
            pl.when(when)(copy.start)
        pending.append((copy, when))

    def column(o):
        cy = order[o]
        up = has_up & (cy <= y)
        down = has_down & (cy >= y)
        for kv in range(2):
            arrived(kv, x, cy)
            send(forward(kv, x, cy, y_sem.at[kv, o, 0], (b, (y + 1) * NX + x)), up)
            send(forward(kv, x, cy, y_sem.at[kv, o, 1], (b, (y - 1) * NX + x)), down)
            send(forward(kv, x, cy, x_sem.at[kv, o, 0], (b, y * NX + xr)))
            send(forward(kv, x, cy, x_sem.at[kv, o, 1], (b, y * NX + xl)))

    def relay(o):
        cy = order[o]
        arrived(0, xl, cy)
        send(forward(0, xl, cy, f_sem.at[o, 0], (b, y * NX + xr)))
        arrived(1, xr, cy)
        send(forward(1, xr, cy, f_sem.at[o, 1], (b, y * NX + xl)))

    def prepare():
        for copy in loads:
            copy.wait()
        lane = lax.broadcasted_iota(jnp.int32, (8, 128), 1)
        lengths = jnp.broadcast_to(dls[...], (8, 128))
        ends = lengths
        step = 1
        while step < 128:
            ends = ends + jnp.where(lane >= step, pltpu.roll(ends, step, axis=1), 0)
            step *= 2
        starts = (ends - lengths).astype(jnp.float32)
        starts = jnp.broadcast_to(starts[0:1, :], (128, 128)).T
        first = b * rows * NX * NY + inner * rows
        qpos = (first + lax.broadcasted_iota(jnp.int32, (128, 128), 1)).astype(jnp.float32)
        begin = jnp.max(jnp.where(starts <= qpos, starts, 0.0), axis=0, keepdims=True)
        key_first = ((b - 1) * rows * NX * NY).astype(jnp.float32)
        limit = jnp.where(b == 0, jnp.float32(1e9), begin - key_first)
        thr[...] = jnp.broadcast_to(limit, (8, 128))
        for h in range(heads):
            g, j = h // group, h % group
            cols = pl.ds(j * rows, rows)
            m_ref[g, :, cols] = jnp.broadcast_to(ams[h : h + 1, :] * LOG2E, (8, rows))
            total = jnp.broadcast_to(ass[h : h + 1, :], (8, rows))
            l_ref[g, :, cols] = total * 0.125
            old = aos[:, pl.ds(h * HD, HD)].astype(jnp.float32).T
            acc[g, :, cols] = old * ass[h : h + 1, :]

    scale = LOG2E / math.sqrt(HD)

    def unit(cx, first, count):
        keys = count * rows
        for part in range(count):
            cy = first + part
            true_y = jnp.where(turn_in, NY - 1 - cy, cy)
            base = (true_y * NX + cx) * rows
            kpos = (base + lax.broadcasted_iota(jnp.int32, (rows, 128), 0)).astype(jnp.float32)
            bias[pl.ds(part * rows, rows), :] = jnp.where(kpos >= thr[0:1, :], 0.0, NEG)

        def head(g, carry):
            cols = pl.ds(pl.multiple_of(g * HD, HD), HD)
            kt = kbuf[cx, pl.ds(first, count), :, cols].reshape(keys, HD)
            vt = vbuf[cx, pl.ds(first, count), :, cols].reshape(keys, HD).T
            scores, weights, shrinks = {}, {}, {}

            def stage_scores(j):
                scores[j] = lax.dot_general(
                    kt, qs[g, pl.ds(j * rows, rows), :], (((1,), (1,)), ((), ())),
                    preferred_element_type=jnp.float32,
                )

            def stage_softmax(j):
                lanes = pl.ds(j * rows, rows)
                st = scores.pop(j) * scale + bias[pl.ds(0, keys), :]
                old = m_ref[g, :, lanes]
                top = jnp.maximum(old, jnp.max(st, axis=0, keepdims=True))
                shrink = jnp.exp2(old - top)
                p = jnp.exp2(st - top[0:1, :])
                part = jnp.sum(p.reshape(keys // 8, 8, rows), axis=0)
                l_ref[g, :, lanes] = l_ref[g, :, lanes] * shrink + part
                m_ref[g, :, lanes] = top
                weights[j] = p.astype(jnp.bfloat16)
                shrinks[j] = shrink

            def stage_mix(j):
                lanes = pl.ds(j * rows, rows)
                mixed = jnp.dot(vt, weights.pop(j), preferred_element_type=jnp.float32)
                acc[g, :, lanes] = acc[g, :, lanes] * shrinks.pop(j)[0:1, :] + mixed

            for j in range(group + 2):
                if j < group:
                    stage_scores(j)
                if 1 <= j <= group:
                    stage_softmax(j - 1)
                if j >= 2:
                    stage_mix(j - 2)
            return carry

        lax.fori_loop(0, kv_heads, head, 0)

    h0 = y // 2 * 2
    h1 = 2 - h0

    prepare()
    column(0)
    column(1)
    relay(0)
    for copy in q_loads:
        copy.wait()
    unit(x, h0, 2)
    column(2)
    relay(1)
    column(3)
    relay(2)
    unit(x, h1, 2)
    relay(3)
    for o in range(NY):
        arrived(1, xl, order[o])
    unit(xl, 0, NY)
    for o in range(NY):
        arrived(0, xr, order[o])
    unit(xr, 0, NY)
    for o in (0, 1):
        arrived(0, xo, order[o])
        arrived(1, xo, order[o])
    unit(xo, h0, 2)
    for o in (2, 3):
        arrived(0, xo, order[o])
        arrived(1, xo, order[o])
    unit(xo, h1, 2)

    outs = []
    for g in range(kv_heads):
        total = jnp.sum(l_ref[g], axis=0, keepdims=True)
        inverse = 1.0 / total
        for j in range(group):
            h = g * group + j
            cols = pl.ds(j * rows, rows)
            ass[h : h + 1, :] = total[:, j * rows : (j + 1) * rows]
            ams[h : h + 1, :] = m_ref[g, 0:1, cols] * (1.0 / LOG2E)
            done = acc[g, :, cols] * inverse[:, j * rows : (j + 1) * rows]
            aos[:, pl.ds(h * HD, HD)] = done.T.astype(jnp.bfloat16)
        span = pl.ds(g * group * HD, group * HD)
        outs.append(pltpu.make_async_copy(aos.at[:, span], o_hbm.at[:, span], out_sem.at[g]))
        outs[-1].start()
    outs.append(pltpu.make_async_copy(ams, nm_hbm, out_sem.at[kv_heads]))
    outs[-1].start()
    outs.append(pltpu.make_async_copy(ass, ns_hbm, out_sem.at[kv_heads + 1]))
    outs[-1].start()
    for copy in z_copies:
        copy.wait_send()
    for copy, when in pending:
        if when is None:
            copy.wait_send()
        else:
            pl.when(when)(copy.wait_send)
    for copy in outs:
        copy.wait()


def body(queries, keys, values, acc_out, acc_max, acc_sum, doc_lengths):
    rows, width = queries.shape
    heads = acc_max.shape[1]
    kv_heads = keys.shape[1] // HD
    wide = heads // kv_heads * rows
    anywhere = pl.BlockSpec(memory_space=pl.ANY)
    out, top, total = pl.pallas_call(
        kernel,
        out_shape=(
            jax.ShapeDtypeStruct((rows, width), jnp.bfloat16),
            jax.ShapeDtypeStruct((heads, rows), jnp.float32),
            jax.ShapeDtypeStruct((heads, rows), jnp.float32),
        ),
        in_specs=[pl.BlockSpec(memory_space=pltpu.HBM)] * 7,
        out_specs=(anywhere,) * 3,
        scratch_shapes=[
            pltpu.VMEM((kv_heads, wide, HD), jnp.bfloat16),
            pltpu.VMEM((rows, width), jnp.bfloat16),
            pltpu.VMEM((heads, rows), jnp.float32),
            pltpu.VMEM((heads, rows), jnp.float32),
            pltpu.VMEM((1, 128), jnp.int32),
            pltpu.VMEM((NX, NY, rows, kv_heads * HD), jnp.bfloat16),
            pltpu.VMEM((NX, NY, rows, kv_heads * HD), jnp.bfloat16),
            pltpu.VMEM((kv_heads, HD, wide), jnp.float32),
            pltpu.VMEM((kv_heads, 8, wide), jnp.float32),
            pltpu.VMEM((kv_heads, 8, wide), jnp.float32),
            pltpu.VMEM((NY * rows, 128), jnp.float32),
            pltpu.VMEM((8, 128), jnp.float32),
            pltpu.SemaphoreType.DMA((4,)),
            pltpu.SemaphoreType.DMA((heads,)),
            pltpu.SemaphoreType.DMA((2, NX, NY)),
            pltpu.SemaphoreType.DMA((2,)),
            pltpu.SemaphoreType.DMA((2, NY, 2)),
            pltpu.SemaphoreType.DMA((2, NY, 2)),
            pltpu.SemaphoreType.DMA((NY, 2)),
            pltpu.SemaphoreType.DMA((kv_heads + 2,)),
        ],
        compiler_params=pltpu.CompilerParams(
            collective_id=0, has_side_effects=True, vmem_limit_bytes=48 << 20
        ),
        name="gather_attend",
    )(*[pltpu.with_memory_space_constraint(t, pltpu.HBM) for t in (queries, keys, values, acc_out, acc_max.T, acc_sum.T, doc_lengths.reshape(1, -1))])
    return out, top.T, total.T


def solution(mesh):
    spec = P(("outer", "inner"), None)
    return jax.shard_map(
        body,
        mesh=mesh,
        in_specs=(spec,) * 6 + (P(),),
        out_specs=(spec,) * 3,
        check_vma=False,
    )
```

```python
import functools
import math

import jax
import jax.numpy as jnp
from jax import lax
from jax.experimental import pallas as pl
from jax.experimental.pallas import tpu as pltpu
from jax.sharding import PartitionSpec as P

HD = 128
NEG = -1e30
LOG2E = math.log2(math.e)
MESH = pl.DeviceIdType.MESH
NX = 4
NY = 4


def kernel(
    q_hbm, k_hbm, v_hbm, ao_hbm, am_hbm, as_hbm, dl_hbm,
    o_ref, nm_ref, ns_ref,
    qs, aos, ams, ass, dls, kbuf, vbuf, acc, m_ref, l_ref, bias, thr,
    in_sem, q_sem, recv_sem, z_sem, y_sem, x_sem, f_sem,
):
    rows = k_hbm.shape[0]
    kv_heads = k_hbm.shape[1] // HD
    heads = q_hbm.shape[1] // HD
    group = heads // kv_heads
    wide = group * rows
    n_outer = lax.axis_size("outer")
    half_outer = n_outer // 2
    b = lax.axis_index("outer")
    inner = lax.axis_index("inner")
    y = inner // NX
    x = inner % NX
    xr = (x + 1) % NX
    xl = (x + NX - 1) % NX
    xo = (x + 2) % NX
    nxt = (b + 1) % n_outer
    prv = (b + n_outer - 1) % n_outer
    turn_out = nxt % half_outer == 0
    turn_in = b % half_outer == 0
    y_out = jnp.where(turn_out, NY - 1 - y, y)
    y_in = jnp.where(turn_in, NY - 1 - y, y)
    has_up = y < NY - 1
    has_down = y > 0
    fed = b > 0
    feeds = b < n_outer - 1

    barrier = pltpu.get_barrier_semaphore()

    def greet(device):
        pl.semaphore_signal(barrier, inc=1, device_id=device, device_id_type=MESH)

    def meet():
        greet((prv, y_in * NX + x))
        greet((b, y * NX + xr))
        greet((b, y * NX + xl))
        pl.when(has_up)(lambda: greet((b, (y + 1) * NX + x)))
        pl.when(has_down)(lambda: greet((b, (y - 1) * NX + x)))

    pl.when(fed)(meet)

    peers = jnp.where(fed, 2 + has_up.astype(jnp.int32) + has_down.astype(jnp.int32), 0)
    pl.semaphore_wait(barrier, peers + feeds.astype(jnp.int32))

    bufs = (kbuf, vbuf)
    sources = (k_hbm, v_hbm)

    z_copies = [
        pltpu.make_async_remote_copy(
            src_ref=sources[kv],
            dst_ref=bufs[kv].at[x, y_out],
            send_sem=z_sem.at[kv],
            recv_sem=recv_sem.at[kv, x, y_out],
            device_id=(nxt, y_out * NX + x),
            device_id_type=MESH,
        )
        for kv in range(2)
    ]

    def feed():
        for copy in z_copies:
            copy.start()

    pl.when(feeds)(feed)

    loads = [
        pltpu.make_async_copy(dl_hbm, dls, in_sem.at[0]),
        pltpu.make_async_copy(am_hbm, ams, in_sem.at[1]),
        pltpu.make_async_copy(as_hbm, ass, in_sem.at[2]),
        pltpu.make_async_copy(ao_hbm, aos, in_sem.at[3]),
    ]
    for copy in loads:
        copy.start()
    q_loads = []
    for h in range(heads):
        q_loads.append(
            pltpu.make_async_copy(
                q_hbm.at[:, pl.ds(h * HD, HD)],
                qs.at[h // group, pl.ds((h % group) * rows, rows), :],
                q_sem.at[h],
            )
        )
        q_loads[-1].start()

    def forward(kv, cx, cy, sem, device):
        return pltpu.make_async_remote_copy(
            src_ref=bufs[kv].at[cx, cy],
            dst_ref=bufs[kv].at[cx, cy],
            send_sem=sem,
            recv_sem=recv_sem.at[kv, cx, cy],
            device_id=device,
            device_id_type=MESH,
        )

    def arrived(kv, cx, cy):
        pltpu.make_async_copy(
            bufs[kv].at[cx, cy], bufs[kv].at[cx, cy], recv_sem.at[kv, cx, cy]
        ).wait()

    def pick(values):
        return jnp.where(
            y == 0, values[0], jnp.where(y == 1, values[1], jnp.where(y == 2, values[2], values[3]))
        )

    order = (y, pick((1, 0, 3, 2)), pick((2, 2, 1, 1)), pick((3, 3, 0, 0)))
    pending = []

    def send(copy, when=None):
        if when is None:
            copy.start()
        else:
            pl.when(when)(copy.start)
        pending.append((copy, when))

    def column(o):
        cy = order[o]
        up = has_up & (cy <= y)
        down = has_down & (cy >= y)
        for kv in range(2):
            arrived(kv, x, cy)
            send(forward(kv, x, cy, y_sem.at[kv, o, 0], (b, (y + 1) * NX + x)), up)
            send(forward(kv, x, cy, y_sem.at[kv, o, 1], (b, (y - 1) * NX + x)), down)
            send(forward(kv, x, cy, x_sem.at[kv, o, 0], (b, y * NX + xr)))
            send(forward(kv, x, cy, x_sem.at[kv, o, 1], (b, y * NX + xl)))

    def relay(o):
        cy = order[o]
        arrived(0, xl, cy)
        send(forward(0, xl, cy, f_sem.at[o, 0], (b, y * NX + xr)))
        arrived(1, xr, cy)
        send(forward(1, xr, cy, f_sem.at[o, 1], (b, y * NX + xl)))

    def prepare():
        for copy in loads:
            copy.wait()
        lane = lax.broadcasted_iota(jnp.int32, (8, 128), 1)
        lengths = jnp.broadcast_to(dls[...], (8, 128))
        ends = lengths
        step = 1
        while step < 128:
            ends = ends + jnp.where(lane >= step, pltpu.roll(ends, step, axis=1), 0)
            step *= 2
        starts = (ends - lengths).astype(jnp.float32)
        starts = jnp.broadcast_to(starts[0:1, :], (128, 128)).T
        first = b * rows * NX * NY + inner * rows
        qpos = (first + lax.broadcasted_iota(jnp.int32, (128, 128), 1)).astype(jnp.float32)
        begin = jnp.max(jnp.where(starts <= qpos, starts, 0.0), axis=0, keepdims=True)
        key_first = ((b - 1) * rows * NX * NY).astype(jnp.float32)
        limit = jnp.where(b == 0, jnp.float32(1e9), begin - key_first)
        thr[...] = jnp.broadcast_to(limit, (8, 128))
        for h in range(heads):
            g, j = h // group, h % group
            cols = pl.ds(j * rows, rows)
            m_ref[g, :, cols] = jnp.broadcast_to(ams[h : h + 1, :] * LOG2E, (8, rows))
            total = jnp.broadcast_to(ass[h : h + 1, :], (8, rows))
            l_ref[g, :, cols] = total * 0.125
            old = aos[:, pl.ds(h * HD, HD)].astype(jnp.float32).T
            acc[g, :, cols] = old * ass[h : h + 1, :]

    scale = LOG2E / math.sqrt(HD)

    def unit(parts, g_first=0, g_last=None):
        keys = len(parts) * 2 * rows

        def set_bias():
            for n, (cx, first) in enumerate(parts):
                for half in range(2):
                    cy = first + half
                    true_y = jnp.where(turn_in, NY - 1 - cy, cy)
                    base = (true_y * NX + cx) * rows
                    kpos = base + lax.broadcasted_iota(jnp.int32, (rows, 128), 0)
                    bias[pl.ds((n * 2 + half) * rows, rows), :] = jnp.where(
                        kpos.astype(jnp.float32) >= thr[0:1, :], 0.0, NEG
                    )

        if g_first == 0:
            set_bias()

        def rows_of(buf, cols):
            tiles = [buf[cx, pl.ds(first, 2), :, cols].reshape(2 * rows, HD) for cx, first in parts]
            return tiles[0] if len(tiles) == 1 else jnp.concatenate(tiles, axis=0)

        def head(g, carry):
            cols = pl.ds(pl.multiple_of(g * HD, HD), HD)
            kt = rows_of(kbuf, cols)
            vt = rows_of(vbuf, cols).T
            scores, weights, shrinks = {}, {}, {}

            def stage_scores(j):
                scores[j] = lax.dot_general(
                    kt, qs[g, pl.ds(j * rows, rows), :], (((1,), (1,)), ((), ())),
                    preferred_element_type=jnp.float32,
                )

            def stage_softmax(j):
                lanes = pl.ds(j * rows, rows)
                st = scores.pop(j) * scale + bias[pl.ds(0, keys), :]
                old = m_ref[g, :, lanes]
                top = jnp.maximum(old, jnp.max(st, axis=0, keepdims=True))
                shrink = jnp.exp2(old - top)
                p = jnp.exp2(st - top[0:1, :])
                part = jnp.sum(p.reshape(keys // 8, 8, rows), axis=0)
                l_ref[g, :, lanes] = l_ref[g, :, lanes] * shrink + part
                m_ref[g, :, lanes] = top
                weights[j] = p.astype(jnp.bfloat16)
                shrinks[j] = shrink

            def stage_mix(j):
                lanes = pl.ds(j * rows, rows)
                mixed = jnp.dot(vt, weights.pop(j), preferred_element_type=jnp.float32)
                acc[g, :, lanes] = acc[g, :, lanes] * shrinks.pop(j)[0:1, :] + mixed

            for j in range(group + 2):
                if j < group:
                    stage_scores(j)
                if 1 <= j <= group:
                    stage_softmax(j - 1)
                if j >= 2:
                    stage_mix(j - 2)
            return carry

        lax.fori_loop(g_first, kv_heads if g_last is None else g_last, head, 0)

    prepare()
    for copy in q_loads:
        copy.wait()

    def attend():
        h0 = y // 2 * 2
        h1 = 2 - h0
        column(0)
        column(1)
        relay(0)
        unit([(x, h0)], 0, 1)
        column(2)
        unit([(x, h0)], 1, 2)
        relay(1)
        unit([(x, h0)], 2, 3)
        column(3)
        unit([(x, h0)], 3, 4)
        arrived(1, xl, order[0])
        arrived(1, xl, order[1])
        arrived(0, xr, order[0])
        arrived(0, xr, order[1])
        unit([(xl, h0), (xr, h0)], 0, 1)
        relay(2)
        unit([(xl, h0), (xr, h0)], 1, 4)
        arrived(0, xo, order[0])
        arrived(1, xo, order[0])
        arrived(0, xo, order[1])
        arrived(1, xo, order[1])
        unit([(x, h1), (xo, h0)], 0, 1)
        relay(3)
        unit([(x, h1), (xo, h0)], 1, 4)
        arrived(1, xl, order[2])
        arrived(1, xl, order[3])
        arrived(0, xr, order[2])
        arrived(0, xr, order[3])
        unit([(xl, h1), (xr, h1)])
        arrived(0, xo, order[2])
        arrived(1, xo, order[2])
        arrived(0, xo, order[3])
        arrived(1, xo, order[3])
        unit([(xo, h1)])
        for copy, when in pending:
            if when is None:
                copy.wait_send()
            else:
                pl.when(when)(copy.wait_send)

    pl.when(fed)(attend)

    for g in range(kv_heads):
        total = jnp.sum(l_ref[g], axis=0, keepdims=True)
        inverse = 1.0 / total
        for j in range(group):
            h = g * group + j
            cols = pl.ds(j * rows, rows)
            ns_ref[h : h + 1, :] = total[:, j * rows : (j + 1) * rows]
            nm_ref[h : h + 1, :] = m_ref[g, 0:1, cols] * (1.0 / LOG2E)
            done = acc[g, :, cols] * inverse[:, j * rows : (j + 1) * rows]
            o_ref[:, pl.ds(h * HD, HD)] = done.T.astype(jnp.bfloat16)

    def fed_next():
        for copy in z_copies:
            copy.wait_send()

    pl.when(feeds)(fed_next)


def body(queries, keys, values, acc_out, acc_max, acc_sum, doc_lengths):
    rows, width = queries.shape
    heads = acc_max.shape[1]
    kv_heads = keys.shape[1] // HD
    wide = heads // kv_heads * rows
    anywhere = pl.BlockSpec(memory_space=pl.ANY)
    out, top, total = pl.pallas_call(
        kernel,
        out_shape=(
            jax.ShapeDtypeStruct((rows, width), jnp.bfloat16),
            jax.ShapeDtypeStruct((heads, rows), jnp.float32),
            jax.ShapeDtypeStruct((heads, rows), jnp.float32),
        ),
        in_specs=[pl.BlockSpec(memory_space=pltpu.HBM)] * 7,
        out_specs=(pl.BlockSpec(memory_space=pltpu.VMEM),) * 3,
        scratch_shapes=[
            pltpu.VMEM((kv_heads, wide, HD), jnp.bfloat16),
            pltpu.VMEM((rows, width), jnp.bfloat16),
            pltpu.VMEM((heads, rows), jnp.float32),
            pltpu.VMEM((heads, rows), jnp.float32),
            pltpu.VMEM((1, 128), jnp.int32),
            pltpu.VMEM((NX, NY, rows, kv_heads * HD), jnp.bfloat16),
            pltpu.VMEM((NX, NY, rows, kv_heads * HD), jnp.bfloat16),
            pltpu.VMEM((kv_heads, HD, wide), jnp.float32),
            pltpu.VMEM((kv_heads, 8, wide), jnp.float32),
            pltpu.VMEM((kv_heads, 8, wide), jnp.float32),
            pltpu.VMEM((NY * rows, 128), jnp.float32),
            pltpu.VMEM((8, 128), jnp.float32),
            pltpu.SemaphoreType.DMA((4,)),
            pltpu.SemaphoreType.DMA((heads,)),
            pltpu.SemaphoreType.DMA((2, NX, NY)),
            pltpu.SemaphoreType.DMA((2,)),
            pltpu.SemaphoreType.DMA((2, NY, 2)),
            pltpu.SemaphoreType.DMA((2, NY, 2)),
            pltpu.SemaphoreType.DMA((NY, 2)),
        ],
        compiler_params=pltpu.CompilerParams(
            collective_id=0, has_side_effects=True, vmem_limit_bytes=48 << 20
        ),
        name="gather_attend",
    )(*[pltpu.with_memory_space_constraint(t, pltpu.HBM) for t in (queries, keys, values, acc_out, acc_max.T, acc_sum.T, doc_lengths.reshape(1, -1))])
    return out, top.T, total.T


def solution(mesh):
    spec = P(("outer", "inner"), None)
    return jax.shard_map(
        body,
        mesh=mesh,
        in_specs=(spec,) * 6 + (P(),),
        out_specs=(spec,) * 3,
        check_vma=False,
    )
```

```python
import functools
import math

import jax
import jax.numpy as jnp
from jax import lax
from jax.experimental import pallas as pl
from jax.experimental.pallas import tpu as pltpu
from jax.sharding import PartitionSpec as P

HD = 128
NEG = -1e30
LOG2E = math.log2(math.e)
MESH = pl.DeviceIdType.MESH
NX = 4
NY = 4


def kernel(
    q_hbm, k_hbm, v_hbm, ao_hbm, am_hbm, as_hbm, dl_hbm,
    o_ref, st_ref,
    qs, aos, ams, ass, dls, kbuf, vbuf, acc, m_ref, l_ref, bias, thr,
    in_sem, q_sem, recv_sem, z_sem, y_sem, x_sem, f_sem,
):
    rows = k_hbm.shape[0]
    kv_heads = k_hbm.shape[1] // HD
    heads = q_hbm.shape[1] // HD
    group = heads // kv_heads
    wide = group * rows
    n_outer = lax.axis_size("outer")
    half_outer = n_outer // 2
    b = lax.axis_index("outer")
    inner = lax.axis_index("inner")
    y = inner // NX
    x = inner % NX
    xr = (x + 1) % NX
    xl = (x + NX - 1) % NX
    xo = (x + 2) % NX
    nxt = (b + 1) % n_outer
    prv = (b + n_outer - 1) % n_outer
    turn_out = nxt % half_outer == 0
    turn_in = b % half_outer == 0
    y_out = jnp.where(turn_out, NY - 1 - y, y)
    y_in = jnp.where(turn_in, NY - 1 - y, y)
    has_up = y < NY - 1
    has_down = y > 0
    fed = b > 0
    feeds = b < n_outer - 1

    barrier = pltpu.get_barrier_semaphore()

    def greet(device):
        pl.semaphore_signal(barrier, inc=1, device_id=device, device_id_type=MESH)

    def meet():
        greet((prv, y_in * NX + x))
        greet((b, y * NX + xr))
        greet((b, y * NX + xl))
        pl.when(has_up)(lambda: greet((b, (y + 1) * NX + x)))
        pl.when(has_down)(lambda: greet((b, (y - 1) * NX + x)))

    pl.when(fed)(meet)

    peers = jnp.where(fed, 2 + has_up.astype(jnp.int32) + has_down.astype(jnp.int32), 0)
    pl.semaphore_wait(barrier, peers + feeds.astype(jnp.int32))

    bufs = (kbuf, vbuf)
    sources = (k_hbm, v_hbm)

    z_copies = [
        pltpu.make_async_remote_copy(
            src_ref=sources[kv],
            dst_ref=bufs[kv].at[x, y_out],
            send_sem=z_sem.at[kv],
            recv_sem=recv_sem.at[kv, x, y_out],
            device_id=(nxt, y_out * NX + x),
            device_id_type=MESH,
        )
        for kv in range(2)
    ]

    def feed():
        for copy in z_copies:
            copy.start()

    pl.when(feeds)(feed)

    loads = [
        pltpu.make_async_copy(dl_hbm, dls, in_sem.at[0]),
        pltpu.make_async_copy(am_hbm, ams, in_sem.at[1]),
        pltpu.make_async_copy(as_hbm, ass, in_sem.at[2]),
        pltpu.make_async_copy(ao_hbm, aos, in_sem.at[3]),
    ]
    for copy in loads:
        copy.start()
    q_loads = []
    for h in range(heads):
        q_loads.append(
            pltpu.make_async_copy(
                q_hbm.at[:, pl.ds(h * HD, HD)],
                qs.at[h // group, pl.ds((h % group) * rows, rows), :],
                q_sem.at[h],
            )
        )
        q_loads[-1].start()

    def forward(kv, cx, cy, sem, device):
        return pltpu.make_async_remote_copy(
            src_ref=bufs[kv].at[cx, cy],
            dst_ref=bufs[kv].at[cx, cy],
            send_sem=sem,
            recv_sem=recv_sem.at[kv, cx, cy],
            device_id=device,
            device_id_type=MESH,
        )

    def arrived(kv, cx, cy):
        pltpu.make_async_copy(
            bufs[kv].at[cx, cy], bufs[kv].at[cx, cy], recv_sem.at[kv, cx, cy]
        ).wait()

    def pick(values):
        return jnp.where(
            y == 0, values[0], jnp.where(y == 1, values[1], jnp.where(y == 2, values[2], values[3]))
        )

    order = (y, pick((1, 0, 3, 2)), pick((2, 2, 1, 1)), pick((3, 3, 0, 0)))
    pending = []

    def send(copy, when=None):
        if when is None:
            copy.start()
        else:
            pl.when(when)(copy.start)
        pending.append((copy, when))

    def column(o):
        cy = order[o]
        up = has_up & (cy <= y)
        down = has_down & (cy >= y)
        for kv in range(2):
            arrived(kv, x, cy)
            send(forward(kv, x, cy, y_sem.at[kv, o, 0], (b, (y + 1) * NX + x)), up)
            send(forward(kv, x, cy, y_sem.at[kv, o, 1], (b, (y - 1) * NX + x)), down)
            send(forward(kv, x, cy, x_sem.at[kv, o, 0], (b, y * NX + xr)))
            send(forward(kv, x, cy, x_sem.at[kv, o, 1], (b, y * NX + xl)))

    def relay(o):
        cy = order[o]
        arrived(0, xl, cy)
        send(forward(0, xl, cy, f_sem.at[o, 0], (b, y * NX + xr)))
        arrived(1, xr, cy)
        send(forward(1, xr, cy, f_sem.at[o, 1], (b, y * NX + xl)))

    def prepare():
        for copy in loads:
            copy.wait()
        lane = lax.broadcasted_iota(jnp.int32, (8, 128), 1)
        lengths = jnp.broadcast_to(dls[...], (8, 128))
        ends = lengths
        step = 1
        while step < 128:
            ends = ends + jnp.where(lane >= step, pltpu.roll(ends, step, axis=1), 0)
            step *= 2
        starts = (ends - lengths).astype(jnp.float32)
        starts = jnp.broadcast_to(starts[0:1, :], (128, 128)).T
        first = b * rows * NX * NY + inner * rows
        qpos = (first + lax.broadcasted_iota(jnp.int32, (128, 128), 1)).astype(jnp.float32)
        begin = jnp.max(jnp.where(starts <= qpos, starts, 0.0), axis=0, keepdims=True)
        key_first = ((b - 1) * rows * NX * NY).astype(jnp.float32)
        limit = jnp.where(b == 0, jnp.float32(1e9), begin - key_first)
        thr[...] = jnp.broadcast_to(limit, (8, 128))
        for h in range(heads):
            g, j = h // group, h % group
            cols = pl.ds(j * rows, rows)
            m_ref[g, :, cols] = jnp.broadcast_to(ams[h : h + 1, :] * LOG2E, (8, rows))
            total = jnp.broadcast_to(ass[h : h + 1, :], (8, rows))
            l_ref[g, :, cols] = total * 0.125
            old = aos[:, pl.ds(h * HD, HD)].astype(jnp.float32).T
            acc[g, :, cols] = old * ass[h : h + 1, :]

    scale = LOG2E / math.sqrt(HD)

    def unit(parts, g_first=0, g_last=None):
        keys = sum(count for _, _, count in parts) * rows

        def set_bias():
            slots = [(cx, first + n) for cx, first, count in parts for n in range(count)]
            for n, (cx, cy) in enumerate(slots):
                true_y = jnp.where(turn_in, NY - 1 - cy, cy)
                base = (true_y * NX + cx) * rows
                kpos = base + lax.broadcasted_iota(jnp.int32, (rows, 128), 0)
                bias[pl.ds(n * rows, rows), :] = jnp.where(
                    kpos.astype(jnp.float32) >= thr[0:1, :], 0.0, NEG
                )

        if g_first == 0:
            set_bias()

        def rows_of(buf, cols):
            tiles = [
                buf[cx, pl.ds(first, count), :, cols].reshape(count * rows, HD)
                for cx, first, count in parts
            ]
            return tiles[0] if len(tiles) == 1 else jnp.concatenate(tiles, axis=0)

        def head(g, carry):
            cols = pl.ds(pl.multiple_of(g * HD, HD), HD)
            kt = rows_of(kbuf, cols)
            vt = rows_of(vbuf, cols).T
            scores, weights, shrinks = {}, {}, {}

            def stage_scores(j):
                scores[j] = lax.dot_general(
                    kt, qs[g, pl.ds(j * rows, rows), :], (((1,), (1,)), ((), ())),
                    preferred_element_type=jnp.float32,
                )

            def stage_softmax(j):
                lanes = pl.ds(j * rows, rows)
                st = scores.pop(j) * scale + bias[pl.ds(0, keys), :]
                old = m_ref[g, :, lanes]
                top = jnp.maximum(old, jnp.max(st, axis=0, keepdims=True))
                shrink = jnp.exp2(old - top)
                p = jnp.exp2(st - top[0:1, :])
                part = jnp.sum(p.reshape(keys // 8, 8, rows), axis=0)
                l_ref[g, :, lanes] = l_ref[g, :, lanes] * shrink + part
                m_ref[g, :, lanes] = top
                weights[j] = p.astype(jnp.bfloat16)
                shrinks[j] = shrink

            def stage_mix(j):
                lanes = pl.ds(j * rows, rows)
                mixed = jnp.dot(vt, weights.pop(j), preferred_element_type=jnp.float32)
                acc[g, :, lanes] = acc[g, :, lanes] * shrinks.pop(j)[0:1, :] + mixed

            for j in range(group + 2):
                if j < group:
                    stage_scores(j)
                if 1 <= j <= group:
                    stage_softmax(j - 1)
                if j >= 2:
                    stage_mix(j - 2)
            return carry

        lax.fori_loop(g_first, kv_heads if g_last is None else g_last, head, 0)

    prepare()
    for copy in q_loads:
        copy.wait()

    def attend():
        h0 = y // 2 * 2
        h1 = 2 - h0
        column(0)
        column(1)
        relay(0)
        unit([(x, h0, 2)], 0, 1)
        column(2)
        unit([(x, h0, 2)], 1, 2)
        relay(1)
        unit([(x, h0, 2)], 2, 3)
        column(3)
        unit([(x, h0, 2)], 3, 4)
        arrived(1, xl, order[0])
        arrived(1, xl, order[1])
        arrived(0, xr, order[0])
        arrived(0, xr, order[1])
        unit([(xl, h0, 2), (xr, h0, 2)], 0, 2)
        relay(2)
        unit([(xl, h0, 2), (xr, h0, 2)], 2, 4)
        arrived(0, xo, order[0])
        arrived(1, xo, order[0])
        arrived(0, xo, order[1])
        arrived(1, xo, order[1])
        unit([(x, h1, 2), (xo, h0, 2)], 0, 2)
        relay(3)
        unit([(x, h1, 2), (xo, h0, 2)], 2, 4)
        arrived(1, xl, order[2])
        arrived(1, xl, order[3])
        arrived(0, xr, order[2])
        arrived(0, xr, order[3])
        unit([(xl, h1, 2), (xr, h1, 2)])
        arrived(0, xo, order[2])
        arrived(1, xo, order[2])
        arrived(0, xo, order[3])
        arrived(1, xo, order[3])
        unit([(xo, h1, 2)])
        for copy, when in pending:
            if when is None:
                copy.wait_send()
            else:
                pl.when(when)(copy.wait_send)

    pl.when(fed)(attend)

    for g in range(kv_heads):
        total = jnp.sum(l_ref[g], axis=0, keepdims=True)
        inverse = 1.0 / total
        for j in range(group):
            h = g * group + j
            cols = pl.ds(j * rows, rows)
            st_ref[heads + h : heads + h + 1, :] = total[:, j * rows : (j + 1) * rows]
            st_ref[h : h + 1, :] = m_ref[g, 0:1, cols] * (1.0 / LOG2E)
            done = acc[g, :, cols] * inverse[:, j * rows : (j + 1) * rows]
            o_ref[:, pl.ds(h * HD, HD)] = done.T.astype(jnp.bfloat16)

    def fed_next():
        for copy in z_copies:
            copy.wait_send()

    pl.when(feeds)(fed_next)


def body(queries, keys, values, acc_out, acc_max, acc_sum, doc_lengths):
    rows, width = queries.shape
    heads = acc_max.shape[1]
    kv_heads = keys.shape[1] // HD
    wide = heads // kv_heads * rows
    anywhere = pl.BlockSpec(memory_space=pl.ANY)
    out, stats = pl.pallas_call(
        kernel,
        out_shape=(
            jax.ShapeDtypeStruct((rows, width), jnp.bfloat16),
            jax.ShapeDtypeStruct((2 * heads, rows), jnp.float32),
        ),
        in_specs=[pl.BlockSpec(memory_space=pltpu.HBM)] * 7,
        out_specs=(pl.BlockSpec(memory_space=pltpu.VMEM),) * 2,
        scratch_shapes=[
            pltpu.VMEM((kv_heads, wide, HD), jnp.bfloat16),
            pltpu.VMEM((rows, width), jnp.bfloat16),
            pltpu.VMEM((heads, rows), jnp.float32),
            pltpu.VMEM((heads, rows), jnp.float32),
            pltpu.VMEM((1, 128), jnp.int32),
            pltpu.VMEM((NX, NY, rows, kv_heads * HD), jnp.bfloat16),
            pltpu.VMEM((NX, NY, rows, kv_heads * HD), jnp.bfloat16),
            pltpu.VMEM((kv_heads, HD, wide), jnp.float32),
            pltpu.VMEM((kv_heads, 8, wide), jnp.float32),
            pltpu.VMEM((kv_heads, 8, wide), jnp.float32),
            pltpu.VMEM((NY * rows, 128), jnp.float32),
            pltpu.VMEM((8, 128), jnp.float32),
            pltpu.SemaphoreType.DMA((4,)),
            pltpu.SemaphoreType.DMA((heads,)),
            pltpu.SemaphoreType.DMA((2, NX, NY)),
            pltpu.SemaphoreType.DMA((2,)),
            pltpu.SemaphoreType.DMA((2, NY, 2)),
            pltpu.SemaphoreType.DMA((2, NY, 2)),
            pltpu.SemaphoreType.DMA((NY, 2)),
        ],
        compiler_params=pltpu.CompilerParams(
            collective_id=0, has_side_effects=True, vmem_limit_bytes=48 << 20
        ),
        name="gather_attend",
    )(*[pltpu.with_memory_space_constraint(t, pltpu.HBM) for t in (queries, keys, values, acc_out, acc_max.T, acc_sum.T, doc_lengths.reshape(1, -1))])
    return out, stats[:heads].T, stats[heads:].T


def solution(mesh):
    spec = P(("outer", "inner"), None)
    return jax.shard_map(
        body,
        mesh=mesh,
        in_specs=(spec,) * 6 + (P(),),
        out_specs=(spec,) * 3,
        check_vma=False,
    )
```
